256 devices in a mesh: fsdp: 16 (over y, z_hi, core), tp: 16 (over x, z_lo).
Axes of the slice: x: 4, y: 4, z: 8 (z_hi: 2, z_lo: 4; z = z_hi * 4 + z_lo), core: 2. Of those that a mesh axis runs over, the one named last changes fastest.
Arguments:
- tokens: bfloat16 [16384, 4096], P(('fsdp', 'tp')), may hold values from -6 to 6
- norm_gain: float32 [4096], replicated, may hold values from 0.5 to 2
- up_blocks: bfloat16 [256, 24, 64, 64], P(('tp', 'fsdp')), may hold values from -0.1875 to 0.1875
- up_rows: int32 [256, 24], P(('tp', 'fsdp')), may hold values from 0 to 63, as said below
- up_count: int32 [256], P(('tp', 'fsdp')), may hold values from 12 to 24, as said below
- down_blocks: bfloat16 [16, 64, 6, 64, 64], P('tp', 'fsdp'), may hold values from -0.09375 to 0.09375
- down_rows: int32 [16, 64, 6], P('tp', 'fsdp'), may hold values from 0 to 15, as said below
- down_count: int32 [16, 64], P('tp', 'fsdp'), may hold values from 3 to 6, as said below
Outputs:
- mixed: bfloat16 [16384, 4096], P(('fsdp', 'tp'))
The draws below stay inside these ranges and needn't reach their ends.
Inputs may be any that keep to these rules, and one draw needn't show every extreme that they name: `up_rows`: the slots of one hidden block column name distinct input blocks. `up_count`: some hidden block column has exactly 24 live slots. `down_rows`: the slots of one panel and output block column name distinct hidden blocks of that panel. `down_count`: some panel and output block column has exactly 6 live slots.
All inputs are finite; a program needn't handle non-finite values.
Results may differ from the reference program's by a relative error of at most 0.014.
Values may be sent and summed in bfloat16 or wider, within the bound.
A program may use at most 128 MiB of HBM per device.

```python
import math
import jax
import jax.numpy as jnp
from jax import lax

D = 4096
FF = 16384
BLK = 64
MAXU = 24
MAXD = 6
HB = 16
TOKENS = 16384
N_TP = 16


def draw_up_rows(key, part):
    keys = jax.random.split(jax.random.fold_in(key, 11), FF // BLK)
    perms = jax.vmap(lambda k: jax.random.permutation(k, D // BLK))(keys)
    return perms[:, :MAXU].astype(jnp.int32)


def draw_up_count(key, part):
    first = jax.random.fold_in(key, 12)
    second = jax.random.fold_in(key, 13)
    counts = jax.random.randint(first, (FF // BLK,), MAXU // 2, MAXU + 1)
    chosen = jax.random.randint(second, (), 0, FF // BLK)
    place = jnp.arange(FF // BLK, dtype=jnp.int32)
    return jnp.where(place == chosen, MAXU, counts).astype(jnp.int32)


def draw_down_rows(key, part):
    keys = jax.random.split(jax.random.fold_in(key, 21), N_TP * (D // BLK))
    perms = jax.vmap(lambda k: jax.random.permutation(k, HB))(keys)
    return perms[:, :MAXD].reshape(N_TP, D // BLK, MAXD).astype(jnp.int32)


def draw_down_count(key, part):
    first = jax.random.fold_in(key, 22)
    second = jax.random.fold_in(key, 23)
    counts = jax.random.randint(first, (N_TP * (D // BLK),), MAXD // 2, MAXD + 1)
    chosen = jax.random.randint(second, (), 0, N_TP * (D // BLK))
    place = jnp.arange(N_TP * (D // BLK), dtype=jnp.int32)
    return jnp.where(place == chosen, MAXD, counts).reshape(N_TP, D // BLK).astype(jnp.int32)


def block_scale(key, shape, cuts, low, largest):
    gain = 1.0
    for dim, shards_of in cuts:
        steps = jax.random.uniform(jax.random.fold_in(jax.random.fold_in(key, 6), dim), (shards_of,), jnp.float32, low / len(cuts), largest / len(cuts))
        gain = gain * jnp.repeat(jnp.exp(steps), shape[dim] // shards_of).reshape((-1,) + (1,) * (len(shape) - 1 - dim))
    return gain


def noise(rng, shape, deviation, reach, shards=(), held_as=jnp.bfloat16):
    values = deviation * jax.random.normal(rng, shape, jnp.float32)
    if shards:
        values = values * block_scale(rng, shape, shards, -0.22, 0.18)
    return jnp.clip(values, -reach, reach).astype(held_as)


def setup_inputs(seed: int = 0) -> dict:
    splits = jax.random.split(jax.random.key(seed), 9)
    return {
        "tokens": noise(splits[0], (TOKENS, D), 1.0, 6.0, ((0, 256),)),
        "norm_gain": jnp.clip(jnp.exp(jax.random.uniform(splits[1], (D,), jnp.float32, math.log(0.5), math.log(2.0))), 0.5, 2.0),
        "up_blocks": noise(splits[2], (FF // BLK, MAXU, BLK, BLK), (MAXU * BLK * 3 // 4) ** -0.5, 0.1875, ((0, 256),)),
        "up_rows": draw_up_rows(jax.random.fold_in(splits[8], 71), 0),
        "up_count": draw_up_count(jax.random.fold_in(splits[8], 71), 0),
        "down_blocks": noise(splits[5], (N_TP, D // BLK, MAXD, BLK, BLK), (N_TP * MAXD * BLK * 3 // 4) ** -0.5, 0.09375, ((0, 16), (1, 16))),
        "down_rows": draw_down_rows(jax.random.fold_in(splits[8], 71), 0),
        "down_count": draw_down_count(jax.random.fold_in(splits[8], 71), 0),
    }


def reference(tokens, norm_gain, up_blocks, up_rows, up_count, down_blocks, down_rows, down_count):
    x_float = tokens.astype(jnp.float32)
    scale = lax.rsqrt(lax.optimization_barrier(jnp.mean(x_float * x_float, axis=-1, keepdims=True)) + 1e-05)
    normed = (x_float * scale * norm_gain).astype(jnp.bfloat16)
    total_rows = normed.shape[0]
    normed_blocks = normed.reshape(total_rows, D // BLK, BLK)
    up_slots = jnp.arange(MAXU, dtype=jnp.int32)

    def up_column(packed):
        weights, rows, count = packed
        live = (up_slots < count).astype(jnp.bfloat16)
        masked = weights * live[:, None, None]
        picked = jnp.take(normed_blocks, rows, axis=1)
        return jnp.einsum('tsk,skn->tn', picked.astype(jnp.float32), masked.astype(jnp.float32))
    pre = lax.map(up_column, (up_blocks, up_rows, up_count))
    hidden = jax.nn.gelu(pre, approximate=True).astype(jnp.bfloat16)
    down_slots = jnp.arange(MAXD, dtype=jnp.int32)
    panel_base = (jnp.arange(N_TP, dtype=jnp.int32) * HB)[:, None]

    def down_column(packed):
        weights, rows, count = packed
        live = (down_slots[None, :] < count[:, None]).astype(jnp.bfloat16)
        masked = weights * live[:, :, None, None]
        picked = jnp.take(hidden, (rows + panel_base).astype(jnp.int32), axis=0)
        per_panel = jnp.einsum('psti,psin->ptn', picked.astype(jnp.float32), masked.astype(jnp.float32))
        rounded = per_panel.astype(jnp.bfloat16).astype(jnp.float32)
        return lax.optimization_barrier(jnp.sum(rounded, axis=0))
    branch = lax.map(down_column, (jnp.transpose(down_blocks, (1, 0, 2, 3, 4)), jnp.transpose(down_rows, (1, 0, 2)), jnp.transpose(down_count, (1, 0))))
    branch = jnp.transpose(branch, (1, 0, 2)).reshape(total_rows, D)
    return (x_float + branch).astype(jnp.bfloat16)
```

```python
import jax
import jax.numpy as jnp
from jax import lax
from jax.sharding import PartitionSpec as P

D = 4096
FF = 16384
BLK = 64
LANES = 128


def onehot_dense(weights, rows, span):
    block_ids = jnp.arange(span, dtype=jnp.int32)
    onehot = (rows[:, :, None] == block_ids[None, None, :]).astype(jnp.bfloat16)
    dense = jnp.einsum("csb,cskn->cbkn", onehot, weights, preferred_element_type=jnp.float32)
    return dense.astype(jnp.bfloat16)


def on_device(tokens, norm_gain, up_blocks, up_rows, up_count, down_blocks, down_rows, down_count):
    x_float = tokens.astype(jnp.float32)
    scale = lax.rsqrt(jnp.mean(x_float * x_float, axis=-1, keepdims=True) + 1e-05)
    normed = (x_float * scale * norm_gain).astype(jnp.bfloat16)

    up_slots = up_blocks.shape[1]
    down_cols, down_slots = down_blocks.shape[1], down_blocks.shape[2]
    up_live = (jnp.arange(up_slots, dtype=jnp.int32)[None, :] < up_count[:, None]).astype(jnp.bfloat16)
    down_live = (
        jnp.arange(down_slots, dtype=jnp.int32)[None, None, :] < down_count[:, :, None]
    ).astype(jnp.bfloat16)
    up_w = up_blocks * up_live[:, :, None, None]
    down_w = down_blocks * down_live[:, :, :, None, None]
    n_up = up_w.size
    n_down = down_w.size
    ints = jnp.concatenate(
        [up_rows.reshape(-1), down_rows.reshape(-1)]
    ).astype(jnp.bfloat16)
    n_ints = ints.shape[0]
    pad = (-n_ints) % LANES
    packed = jnp.concatenate(
        [up_w.reshape(-1), down_w.reshape(-1), ints, jnp.zeros((pad,), jnp.bfloat16)]
    ).reshape(1, -1, LANES)
    gathered_w = lax.all_gather(packed, "fsdp", axis=0, tiled=True)
    groups = gathered_w.shape[0]
    flat = gathered_w.reshape(groups, -1)
    up_all = flat[:, :n_up].reshape(groups * up_blocks.shape[0], up_slots, BLK, BLK)
    down_all = flat[:, n_up : n_up + n_down].reshape(groups * down_cols, down_slots, BLK, BLK)
    ints_all = flat[:, n_up + n_down : n_up + n_down + n_ints].astype(jnp.int32)
    up_rows_all = ints_all[:, : up_rows.size].reshape(groups * up_blocks.shape[0], up_slots)
    down_rows_all = ints_all[:, up_rows.size :].reshape(groups * down_cols, down_slots)

    gathered = lax.all_gather(normed, "tp", axis=0, tiled=True)
    total_rows = gathered.shape[0]
    row_blocks = gathered.reshape(total_rows, D // BLK, BLK)

    dense_up = onehot_dense(up_all, up_rows_all, D // BLK)
    pre = jnp.einsum("tbk,cbkn->tcn", row_blocks, dense_up, preferred_element_type=jnp.float32)
    hidden = jax.nn.gelu(pre, approximate=True).astype(jnp.bfloat16)

    panel_span = FF // BLK // lax.axis_size("tp")
    dense_down = onehot_dense(down_all, down_rows_all, panel_span)
    partial_sums = jnp.einsum(
        "thi,jhin->tjn", hidden, dense_down, preferred_element_type=jnp.float32
    ).reshape(total_rows, D)
    summed = lax.psum_scatter(
        partial_sums.astype(jnp.bfloat16), "tp", scatter_dimension=0, tiled=True
    ).astype(jnp.float32)
    return (x_float + summed).astype(jnp.bfloat16)


def solution(mesh):
    placed = (
        P(("fsdp", "tp"), None),
        P(),
        P(("tp", "fsdp"), None, None, None),
        P(("tp", "fsdp"), None),
        P(("tp", "fsdp")),
        P("tp", "fsdp", None, None, None),
        P("tp", "fsdp", None),
        P("tp", "fsdp"),
    )
    return jax.shard_map(
        on_device, mesh=mesh, in_specs=placed, out_specs=P(("fsdp", "tp"), None), check_vma=False
    )
```

```python
import jax
import jax.numpy as jnp
from jax import lax
from jax.sharding import Mesh, PartitionSpec as P

D = 4096
FF = 16384
BLK = 64
LANES = 128


def onehot_dense(weights, rows, span):
    block_ids = jnp.arange(span, dtype=jnp.int32)
    onehot = (rows[:, :, None] == block_ids[None, None, :]).astype(jnp.bfloat16)
    dense = jnp.einsum("csb,cskn->cbkn", onehot, weights, preferred_element_type=jnp.float32)
    return dense.astype(jnp.bfloat16)


def on_device(tokens, norm_gain, up_blocks, up_rows, up_count, down_blocks, down_rows, down_count):
    x_float = tokens.astype(jnp.float32)
    scale = lax.rsqrt(jnp.mean(x_float * x_float, axis=-1, keepdims=True) + 1e-05)
    normed = (x_float * scale * norm_gain).astype(jnp.bfloat16)

    up_slots = up_blocks.shape[1]
    down_cols, down_slots = down_blocks.shape[1], down_blocks.shape[2]
    up_live = (jnp.arange(up_slots, dtype=jnp.int32)[None, :] < up_count[:, None]).astype(jnp.bfloat16)
    down_live = (
        jnp.arange(down_slots, dtype=jnp.int32)[None, None, :] < down_count[:, :, None]
    ).astype(jnp.bfloat16)
    up_w = up_blocks * up_live[:, :, None, None]
    down_w = down_blocks * down_live[:, :, :, None, None]
    n_up = up_w.size
    n_down = down_w.size
    ints = jnp.concatenate(
        [up_rows.reshape(-1), down_rows.reshape(-1)]
    ).astype(jnp.bfloat16)
    n_ints = ints.shape[0]
    pad = (-n_ints) % LANES
    packed = jnp.concatenate(
        [up_w.reshape(-1), down_w.reshape(-1), ints, jnp.zeros((pad,), jnp.bfloat16)]
    ).reshape(1, -1, LANES)
    gathered_w = packed
    for axis in ("core", "zhi", "y"):
        gathered_w = lax.all_gather(gathered_w, axis, axis=0, tiled=True)
    groups = gathered_w.shape[0]
    flat = gathered_w.reshape(groups, -1)
    up_all = flat[:, :n_up].reshape(groups * up_blocks.shape[0], up_slots, BLK, BLK)
    down_all = flat[:, n_up : n_up + n_down].reshape(groups * down_cols, down_slots, BLK, BLK)
    ints_all = flat[:, n_up + n_down : n_up + n_down + n_ints].astype(jnp.int32)
    up_rows_all = ints_all[:, : up_rows.size].reshape(groups * up_blocks.shape[0], up_slots)
    down_rows_all = ints_all[:, up_rows.size :].reshape(groups * down_cols, down_slots)

    gathered = lax.all_gather(normed, "zlo", axis=0, tiled=True)
    gathered = lax.all_gather(gathered, "x", axis=0, tiled=True)
    total_rows = gathered.shape[0]
    row_blocks = gathered.reshape(total_rows, D // BLK, BLK)

    dense_up = onehot_dense(up_all, up_rows_all, D // BLK)
    pre = jnp.einsum("tbk,cbkn->tcn", row_blocks, dense_up, preferred_element_type=jnp.float32)
    hidden = jax.nn.gelu(pre, approximate=True).astype(jnp.bfloat16)

    panel_span = FF // BLK // (lax.axis_size("x") * lax.axis_size("zlo"))
    dense_down = onehot_dense(down_all, down_rows_all, panel_span)
    partial_sums = jnp.einsum(
        "thi,jhin->tjn", hidden, dense_down, preferred_element_type=jnp.float32
    ).reshape(total_rows, D)
    summed = lax.psum_scatter(
        partial_sums.astype(jnp.bfloat16), "x", scatter_dimension=0, tiled=True
    )
    summed = lax.psum_scatter(summed, "zlo", scatter_dimension=0, tiled=True).astype(jnp.float32)
    return (x_float + summed).astype(jnp.bfloat16)


def solution(mesh):
    fsdp = ("y", "zhi", "core")
    tp = ("x", "zlo")
    n_fsdp, n_tp = mesh.shape["fsdp"], mesh.shape["tp"]
    sizes = (n_fsdp // 4, 2, 2, n_tp // 4, 4)
    fine = Mesh(mesh.devices.reshape(sizes), fsdp + tp)
    placed = (
        P(fsdp + tp, None),
        P(),
        P(tp + fsdp, None, None, None),
        P(tp + fsdp, None),
        P(tp + fsdp),
        P(tp, fsdp, None, None, None),
        P(tp, fsdp, None),
        P(tp, fsdp),
    )
    return jax.shard_map(
        on_device, mesh=fine, in_specs=placed, out_specs=P(fsdp + tp, None), check_vma=False
    )
```

```python
import jax
import jax.numpy as jnp
from jax import lax
from jax.sharding import Mesh, PartitionSpec as P

D = 4096
FF = 16384
BLK = 64
LANES = 128


def onehot_dense(weights, rows, span):
    block_ids = jnp.arange(span, dtype=jnp.int32)
    onehot = (rows[:, :, None] == block_ids[None, None, :]).astype(jnp.bfloat16)
    dense = jnp.einsum("csb,cskn->cbkn", onehot, weights, preferred_element_type=jnp.float32)
    return dense.astype(jnp.bfloat16)


def permute_gather(piece, axis):
    size = lax.axis_size(axis)
    me = lax.axis_index(axis)
    whole = jnp.zeros((size,) + piece.shape, piece.dtype)
    whole = lax.dynamic_update_index_in_dim(whole, piece, me, 0)
    for shift in range(1, size):
        moved = lax.ppermute(piece, axis, [(i, (i + shift) % size) for i in range(size)])
        whole = lax.dynamic_update_index_in_dim(whole, moved, (me - shift) % size, 0)
    return whole.reshape((size * piece.shape[0],) + piece.shape[1:])


def on_device(tokens, norm_gain, up_blocks, up_rows, up_count, down_blocks, down_rows, down_count):
    x_float = tokens.astype(jnp.float32)
    scale = lax.rsqrt(jnp.mean(x_float * x_float, axis=-1, keepdims=True) + 1e-05)
    normed = (x_float * scale * norm_gain).astype(jnp.bfloat16)

    up_slots = up_blocks.shape[1]
    down_cols, down_slots = down_blocks.shape[1], down_blocks.shape[2]
    up_live = (jnp.arange(up_slots, dtype=jnp.int32)[None, :] < up_count[:, None]).astype(jnp.bfloat16)
    down_live = (
        jnp.arange(down_slots, dtype=jnp.int32)[None, None, :] < down_count[:, :, None]
    ).astype(jnp.bfloat16)
    up_w = up_blocks * up_live[:, :, None, None]
    down_w = down_blocks * down_live[:, :, :, None, None]
    n_up = up_w.size
    n_down = down_w.size
    ints = jnp.concatenate(
        [up_rows.reshape(-1), down_rows.reshape(-1)]
    ).astype(jnp.bfloat16)
    n_ints = ints.shape[0]
    pad = (-n_ints) % LANES
    packed = jnp.concatenate(
        [up_w.reshape(-1), down_w.reshape(-1), ints, jnp.zeros((pad,), jnp.bfloat16)]
    ).reshape(1, -1, LANES)
    gathered_w = lax.all_gather(packed, "core", axis=0, tiled=True)
    gathered_w = permute_gather(gathered_w, "zhi")
    gathered_w = permute_gather(gathered_w, "y")
    groups = gathered_w.shape[0]
    flat = gathered_w.reshape(groups, -1)
    up_all = flat[:, :n_up].reshape(groups * up_blocks.shape[0], up_slots, BLK, BLK)
    down_all = flat[:, n_up : n_up + n_down].reshape(groups * down_cols, down_slots, BLK, BLK)
    ints_all = flat[:, n_up + n_down : n_up + n_down + n_ints].astype(jnp.int32)
    up_rows_all = ints_all[:, : up_rows.size].reshape(groups * up_blocks.shape[0], up_slots)
    down_rows_all = ints_all[:, up_rows.size :].reshape(groups * down_cols, down_slots)

    gathered = lax.all_gather(normed, "zlo", axis=0, tiled=True)
    gathered = lax.all_gather(gathered, "x", axis=0, tiled=True)
    total_rows = gathered.shape[0]
    row_blocks = gathered.reshape(total_rows, D // BLK, BLK)

    dense_up = onehot_dense(up_all, up_rows_all, D // BLK)
    pre = jnp.einsum("tbk,cbkn->tcn", row_blocks, dense_up, preferred_element_type=jnp.float32)
    hidden = jax.nn.gelu(pre, approximate=True).astype(jnp.bfloat16)

    panel_span = FF // BLK // (lax.axis_size("x") * lax.axis_size("zlo"))
    dense_down = onehot_dense(down_all, down_rows_all, panel_span)
    partial_sums = jnp.einsum(
        "thi,jhin->tjn", hidden, dense_down, preferred_element_type=jnp.float32
    ).reshape(total_rows, D)
    summed = lax.psum_scatter(
        partial_sums.astype(jnp.bfloat16), "x", scatter_dimension=0, tiled=True
    )
    summed = lax.psum_scatter(summed, "zlo", scatter_dimension=0, tiled=True).astype(jnp.float32)
    return (x_float + summed).astype(jnp.bfloat16)


def solution(mesh):
    fsdp = ("y", "zhi", "core")
    tp = ("x", "zlo")
    n_fsdp, n_tp = mesh.shape["fsdp"], mesh.shape["tp"]
    sizes = (n_fsdp // 4, 2, 2, n_tp // 4, 4)
    fine = Mesh(mesh.devices.reshape(sizes), fsdp + tp)
    placed = (
        P(fsdp + tp, None),
        P(),
        P(tp + fsdp, None, None, None),
        P(tp + fsdp, None),
        P(tp + fsdp),
        P(tp, fsdp, None, None, None),
        P(tp, fsdp, None),
        P(tp, fsdp),
    )
    return jax.shard_map(
        on_device, mesh=fine, in_specs=placed, out_specs=P(fsdp + tp, None), check_vma=False
    )
```

```python
import jax
import jax.numpy as jnp
from jax import lax
from jax.sharding import Mesh, PartitionSpec as P

D = 4096
FF = 16384
BLK = 64
LANES = 128


def onehot_dense(weights, rows, span):
    block_ids = jnp.arange(span, dtype=jnp.int32)
    onehot = (rows[:, :, None] == block_ids[None, None, :]).astype(jnp.bfloat16)
    dense = jnp.einsum("csb,cskn->cbkn", onehot, weights, preferred_element_type=jnp.float32)
    return dense.astype(jnp.bfloat16)


def permute_gather(piece, axis):
    size = lax.axis_size(axis)
    me = lax.axis_index(axis)
    whole = jnp.zeros((size,) + piece.shape, piece.dtype)
    whole = lax.dynamic_update_index_in_dim(whole, piece, me, 0)
    for shift in range(1, size):
        moved = lax.ppermute(piece, axis, [(i, (i + shift) % size) for i in range(size)])
        whole = lax.dynamic_update_index_in_dim(whole, moved, (me - shift) % size, 0)
    return whole.reshape((size * piece.shape[0],) + piece.shape[1:])


def on_device(tokens, norm_gain, up_blocks, up_rows, up_count, down_blocks, down_rows, down_count):
    x_float = tokens.astype(jnp.float32)
    scale = lax.rsqrt(jnp.mean(x_float * x_float, axis=-1, keepdims=True) + 1e-05)
    normed = (x_float * scale * norm_gain).astype(jnp.bfloat16)

    up_slots = up_blocks.shape[1]
    down_cols, down_slots = down_blocks.shape[1], down_blocks.shape[2]
    up_live = (jnp.arange(up_slots, dtype=jnp.int32)[None, :] < up_count[:, None]).astype(jnp.bfloat16)
    down_live = (
        jnp.arange(down_slots, dtype=jnp.int32)[None, None, :] < down_count[:, :, None]
    ).astype(jnp.bfloat16)
    up_w = up_blocks * up_live[:, :, None, None]
    down_w = down_blocks * down_live[:, :, :, None, None]
    n_up = up_w.size
    n_down = down_w.size
    ints = jnp.concatenate(
        [up_rows.reshape(-1), down_rows.reshape(-1)]
    ).astype(jnp.bfloat16)
    n_ints = ints.shape[0]
    pad = (-n_ints) % LANES
    packed = jnp.concatenate(
        [up_w.reshape(-1), down_w.reshape(-1), ints, jnp.zeros((pad,), jnp.bfloat16)]
    ).reshape(1, -1, LANES)
    normed, packed = lax.optimization_barrier((normed, packed))
    gathered_w = lax.all_gather(packed, "core", axis=0, tiled=True)
    gathered_w = permute_gather(gathered_w, "zhi")
    gathered_w = permute_gather(gathered_w, "y")
    groups = gathered_w.shape[0]
    flat = gathered_w.reshape(groups, -1)
    up_all = flat[:, :n_up].reshape(groups * up_blocks.shape[0], up_slots, BLK, BLK)
    down_all = flat[:, n_up : n_up + n_down].reshape(groups * down_cols, down_slots, BLK, BLK)
    ints_all = flat[:, n_up + n_down : n_up + n_down + n_ints].astype(jnp.int32)
    up_rows_all = ints_all[:, : up_rows.size].reshape(groups * up_blocks.shape[0], up_slots)
    down_rows_all = ints_all[:, up_rows.size :].reshape(groups * down_cols, down_slots)

    dense_up = onehot_dense(up_all, up_rows_all, D // BLK)
    panel_span = FF // BLK // (lax.axis_size("x") * lax.axis_size("zlo"))
    dense_down = onehot_dense(down_all, down_rows_all, panel_span)

    halves = 2
    part = normed.shape[0] // halves
    outs = []
    for h in range(halves):
        rows = normed[h * part : (h + 1) * part]
        gathered = lax.all_gather(rows, "zlo", axis=0, tiled=True)
        gathered = lax.all_gather(gathered, "x", axis=0, tiled=True)
        total_rows = gathered.shape[0]
        row_blocks = gathered.reshape(total_rows, D // BLK, BLK)
        pre = jnp.einsum("tbk,cbkn->tcn", row_blocks, dense_up, preferred_element_type=jnp.float32)
        hidden = jax.nn.gelu(pre, approximate=True).astype(jnp.bfloat16)
        partial_sums = jnp.einsum(
            "thi,jhin->tjn", hidden, dense_down, preferred_element_type=jnp.float32
        ).reshape(total_rows, D)
        summed = lax.psum_scatter(
            partial_sums.astype(jnp.bfloat16), "x", scatter_dimension=0, tiled=True
        )
        outs.append(lax.psum_scatter(summed, "zlo", scatter_dimension=0, tiled=True))
    summed = jnp.concatenate(outs, axis=0).astype(jnp.float32)
    return (x_float + summed).astype(jnp.bfloat16)


def solution(mesh):
    fsdp = ("y", "zhi", "core")
    tp = ("x", "zlo")
    n_fsdp, n_tp = mesh.shape["fsdp"], mesh.shape["tp"]
    sizes = (n_fsdp // 4, 2, 2, n_tp // 4, 4)
    fine = Mesh(mesh.devices.reshape(sizes), fsdp + tp)
    placed = (
        P(fsdp + tp, None),
        P(),
        P(tp + fsdp, None, None, None),
        P(tp + fsdp, None),
        P(tp + fsdp),
        P(tp, fsdp, None, None, None),
        P(tp, fsdp, None),
        P(tp, fsdp),
    )
    return jax.shard_map(
        on_device, mesh=fine, in_specs=placed, out_specs=P(fsdp + tp, None), check_vma=False
    )
```

```python
import jax
import jax.numpy as jnp
from jax import lax
from jax.sharding import Mesh, PartitionSpec as P

D = 4096
FF = 16384
BLK = 64
LANES = 128


def onehot_dense(weights, rows, span):
    block_ids = jnp.arange(span, dtype=jnp.int32)
    onehot = (rows[:, :, None] == block_ids[None, None, :]).astype(jnp.bfloat16)
    dense = jnp.einsum("csb,cskn->cbkn", onehot, weights, preferred_element_type=jnp.float32)
    return dense.astype(jnp.bfloat16)


def permute_gather(piece, axis):
    size = lax.axis_size(axis)
    me = lax.axis_index(axis)
    whole = jnp.zeros((size,) + piece.shape, piece.dtype)
    whole = lax.dynamic_update_index_in_dim(whole, piece, me, 0)
    for shift in range(1, size):
        moved = lax.ppermute(piece, axis, [(i, (i + shift) % size) for i in range(size)])
        whole = lax.dynamic_update_index_in_dim(whole, moved, (me - shift) % size, 0)
    return whole.reshape((size * piece.shape[0],) + piece.shape[1:])


def on_device(tokens, norm_gain, up_blocks, up_rows, up_count, down_blocks, down_rows, down_count):
    x_float = tokens.astype(jnp.float32)
    scale = lax.rsqrt(jnp.mean(x_float * x_float, axis=-1, keepdims=True) + 1e-05)
    normed = (x_float * scale * norm_gain).astype(jnp.bfloat16)

    up_slots = up_blocks.shape[1]
    down_cols, down_slots = down_blocks.shape[1], down_blocks.shape[2]
    up_live = (jnp.arange(up_slots, dtype=jnp.int32)[None, :] < up_count[:, None]).astype(jnp.bfloat16)
    down_live = (
        jnp.arange(down_slots, dtype=jnp.int32)[None, None, :] < down_count[:, :, None]
    ).astype(jnp.bfloat16)
    up_w = up_blocks * up_live[:, :, None, None]
    down_w = down_blocks * down_live[:, :, :, None, None]
    n_up = up_w.size
    n_down = down_w.size
    ints = jnp.concatenate(
        [up_rows.reshape(-1), down_rows.reshape(-1)]
    ).astype(jnp.bfloat16)
    n_ints = ints.shape[0]
    pad = (-n_ints) % LANES
    packed = jnp.concatenate(
        [up_w.reshape(-1), down_w.reshape(-1), ints, jnp.zeros((pad,), jnp.bfloat16)]
    ).reshape(1, -1, LANES)
    normed, packed = lax.optimization_barrier((normed, packed))
    gathered_w = lax.all_gather(packed, "core", axis=0, tiled=True)
    gathered_w = permute_gather(gathered_w, "zhi")
    gathered_w = permute_gather(gathered_w, "y")
    groups = gathered_w.shape[0]
    flat = gathered_w.reshape(groups, -1)
    up_all = flat[:, :n_up].reshape(groups * up_blocks.shape[0], up_slots, BLK, BLK)
    down_all = flat[:, n_up : n_up + n_down].reshape(groups * down_cols, down_slots, BLK, BLK)
    ints_all = flat[:, n_up + n_down : n_up + n_down + n_ints].astype(jnp.int32)
    up_rows_all = ints_all[:, : up_rows.size].reshape(groups * up_blocks.shape[0], up_slots)
    down_rows_all = ints_all[:, up_rows.size :].reshape(groups * down_cols, down_slots)

    gathered = lax.all_gather(normed, "zlo", axis=0, tiled=True)
    gathered = lax.all_gather(gathered, "x", axis=0, tiled=True)
    total_rows = gathered.shape[0]
    row_blocks = gathered.reshape(total_rows, D // BLK, BLK)

    dense_up = onehot_dense(up_all, up_rows_all, D // BLK)
    pre = jnp.einsum("tbk,cbkn->tcn", row_blocks, dense_up, preferred_element_type=jnp.float32)
    hidden = jax.nn.gelu(pre, approximate=True).astype(jnp.bfloat16)

    panel_span = FF // BLK // (lax.axis_size("x") * lax.axis_size("zlo"))
    dense_down = onehot_dense(down_all, down_rows_all, panel_span)
    partial_sums = jnp.einsum(
        "thi,jhin->tjn", hidden, dense_down, preferred_element_type=jnp.float32
    ).reshape(total_rows, D)
    summed = lax.psum_scatter(
        partial_sums.astype(jnp.bfloat16), "x", scatter_dimension=0, tiled=True
    )
    summed = lax.psum_scatter(summed, "zlo", scatter_dimension=0, tiled=True).astype(jnp.float32)
    return (x_float + summed).astype(jnp.bfloat16)


def solution(mesh):
    fsdp = ("y", "zhi", "core")
    tp = ("x", "zlo")
    n_fsdp, n_tp = mesh.shape["fsdp"], mesh.shape["tp"]
    sizes = (n_fsdp // 4, 2, 2, n_tp // 4, 4)
    fine = Mesh(mesh.devices.reshape(sizes), fsdp + tp)
    placed = (
        P(fsdp + tp, None),
        P(),
        P(tp + fsdp, None, None, None),
        P(tp + fsdp, None),
        P(tp + fsdp),
        P(tp, fsdp, None, None, None),
        P(tp, fsdp, None),
        P(tp, fsdp),
    )
    return jax.shard_map(
        on_device, mesh=fine, in_specs=placed, out_specs=P(fsdp + tp, None), check_vma=False
    )
```

```python
import jax
import jax.numpy as jnp
from jax import lax
from jax.sharding import Mesh, PartitionSpec as P

D = 4096
FF = 16384
BLK = 64
LANES = 128


def onehot_dense(weights, rows, span):
    block_ids = jnp.arange(span, dtype=jnp.int32)
    onehot = (rows[:, :, None] == block_ids[None, None, :]).astype(jnp.bfloat16)
    dense = jnp.einsum("csb,cskn->cbkn", onehot, weights, preferred_element_type=jnp.float32)
    return dense.astype(jnp.bfloat16)


def permute_gather(piece, axis):
    size = lax.axis_size(axis)
    me = lax.axis_index(axis)
    whole = jnp.zeros((size,) + piece.shape, piece.dtype)
    whole = lax.dynamic_update_index_in_dim(whole, piece, me, 0)
    for shift in range(1, size):
        moved = lax.ppermute(piece, axis, [(i, (i + shift) % size) for i in range(size)])
        whole = lax.dynamic_update_index_in_dim(whole, moved, (me - shift) % size, 0)
    return whole.reshape((size * piece.shape[0],) + piece.shape[1:])


def permute_reduce_scatter(whole, axis):
    size = lax.axis_size(axis)
    me = lax.axis_index(axis)
    chunks = whole.reshape((size, whole.shape[0] // size) + whole.shape[1:])
    acc = lax.dynamic_index_in_dim(chunks, me, 0, keepdims=False).astype(jnp.float32)
    for shift in range(1, size):
        send = lax.dynamic_index_in_dim(chunks, (me + shift) % size, 0, keepdims=False)
        moved = lax.ppermute(send, axis, [(i, (i + shift) % size) for i in range(size)])
        acc = acc + moved.astype(jnp.float32)
    return acc


def on_device(tokens, norm_gain, up_blocks, up_rows, up_count, down_blocks, down_rows, down_count):
    x_float = tokens.astype(jnp.float32)
    scale = lax.rsqrt(jnp.mean(x_float * x_float, axis=-1, keepdims=True) + 1e-05)
    normed = (x_float * scale * norm_gain).astype(jnp.bfloat16)

    up_slots = up_blocks.shape[1]
    down_cols, down_slots = down_blocks.shape[1], down_blocks.shape[2]
    up_live = (jnp.arange(up_slots, dtype=jnp.int32)[None, :] < up_count[:, None]).astype(jnp.bfloat16)
    down_live = (
        jnp.arange(down_slots, dtype=jnp.int32)[None, None, :] < down_count[:, :, None]
    ).astype(jnp.bfloat16)
    up_w = up_blocks * up_live[:, :, None, None]
    down_w = down_blocks * down_live[:, :, :, None, None]
    n_up = up_w.size
    n_down = down_w.size
    ints = jnp.concatenate(
        [up_rows.reshape(-1), down_rows.reshape(-1)]
    ).astype(jnp.bfloat16)
    n_ints = ints.shape[0]
    pad = (-n_ints) % LANES
    packed = jnp.concatenate(
        [up_w.reshape(-1), down_w.reshape(-1), ints, jnp.zeros((pad,), jnp.bfloat16)]
    ).reshape(1, -1, LANES)
    gathered_w = lax.all_gather(packed, "core", axis=0, tiled=True)
    gathered_w = permute_gather(gathered_w, "zhi")
    gathered_w = permute_gather(gathered_w, "y")
    groups = gathered_w.shape[0]
    flat = gathered_w.reshape(groups, -1)
    up_all = flat[:, :n_up].reshape(groups * up_blocks.shape[0], up_slots, BLK, BLK)
    down_all = flat[:, n_up : n_up + n_down].reshape(groups * down_cols, down_slots, BLK, BLK)
    ints_all = flat[:, n_up + n_down : n_up + n_down + n_ints].astype(jnp.int32)
    up_rows_all = ints_all[:, : up_rows.size].reshape(groups * up_blocks.shape[0], up_slots)
    down_rows_all = ints_all[:, up_rows.size :].reshape(groups * down_cols, down_slots)

    gathered = lax.all_gather(normed, "zlo", axis=0, tiled=True)
    gathered = lax.all_gather(gathered, "x", axis=0, tiled=True)
    total_rows = gathered.shape[0]
    row_blocks = gathered.reshape(total_rows, D // BLK, BLK)

    dense_up = onehot_dense(up_all, up_rows_all, D // BLK)
    pre = jnp.einsum("tbk,cbkn->tcn", row_blocks, dense_up, preferred_element_type=jnp.float32)
    hidden = jax.nn.gelu(pre, approximate=True).astype(jnp.bfloat16)

    panel_span = FF // BLK // (lax.axis_size("x") * lax.axis_size("zlo"))
    dense_down = onehot_dense(down_all, down_rows_all, panel_span)
    partial_sums = jnp.einsum(
        "thi,jhin->tjn", hidden, dense_down, preferred_element_type=jnp.float32
    ).reshape(total_rows, D)
    summed = lax.psum_scatter(
        partial_sums.astype(jnp.bfloat16), "x", scatter_dimension=0, tiled=True
    )
    summed = permute_reduce_scatter(summed, "zlo")
    return (x_float + summed).astype(jnp.bfloat16)


def solution(mesh):
    fsdp = ("y", "zhi", "core")
    tp = ("x", "zlo")
    n_fsdp, n_tp = mesh.shape["fsdp"], mesh.shape["tp"]
    sizes = (n_fsdp // 4, 2, 2, n_tp // 4, 4)
    fine = Mesh(mesh.devices.reshape(sizes), fsdp + tp)
    placed = (
        P(fsdp + tp, None),
        P(),
        P(tp + fsdp, None, None, None),
        P(tp + fsdp, None),
        P(tp + fsdp),
        P(tp, fsdp, None, None, None),
        P(tp, fsdp, None),
        P(tp, fsdp),
    )
    return jax.shard_map(
        on_device, mesh=fine, in_specs=placed, out_specs=P(fsdp + tp, None), check_vma=False
    )
```

```python
import jax
import jax.numpy as jnp
from jax import lax
from jax.sharding import Mesh, PartitionSpec as P

D = 4096
FF = 16384
BLK = 64
LANES = 128


def onehot_dense(weights, rows, span):
    block_ids = jnp.arange(span, dtype=jnp.int32)
    onehot = (rows[:, :, None] == block_ids[None, None, :]).astype(jnp.bfloat16)
    dense = jnp.einsum("csb,cskn->cbkn", onehot, weights, preferred_element_type=jnp.float32)
    return dense.astype(jnp.bfloat16)


def permute_gather(piece, axis):
    size = lax.axis_size(axis)
    me = lax.axis_index(axis)
    whole = jnp.zeros((size,) + piece.shape, piece.dtype)
    whole = lax.dynamic_update_index_in_dim(whole, piece, me, 0)
    for shift in range(1, size):
        moved = lax.ppermute(piece, axis, [(i, (i + shift) % size) for i in range(size)])
        whole = lax.dynamic_update_index_in_dim(whole, moved, (me - shift) % size, 0)
    return whole.reshape((size * piece.shape[0],) + piece.shape[1:])


def permute_reduce_scatter(whole, axis):
    size = lax.axis_size(axis)
    me = lax.axis_index(axis)
    chunks = whole.reshape((size, whole.shape[0] // size) + whole.shape[1:])
    acc = lax.dynamic_index_in_dim(chunks, me, 0, keepdims=False).astype(jnp.float32)
    for shift in range(1, size):
        send = lax.dynamic_index_in_dim(chunks, (me + shift) % size, 0, keepdims=False)
        moved = lax.ppermute(send, axis, [(i, (i + shift) % size) for i in range(size)])
        acc = acc + moved.astype(jnp.float32)
    return acc


def on_device(tokens, norm_gain, up_blocks, up_rows, up_count, down_blocks, down_rows, down_count):
    x_float = tokens.astype(jnp.float32)
    scale = lax.rsqrt(jnp.mean(x_float * x_float, axis=-1, keepdims=True) + 1e-05)
    normed = (x_float * scale * norm_gain).astype(jnp.bfloat16)

    up_slots = up_blocks.shape[1]
    down_cols, down_slots = down_blocks.shape[1], down_blocks.shape[2]
    up_live = (jnp.arange(up_slots, dtype=jnp.int32)[None, :] < up_count[:, None]).astype(jnp.bfloat16)
    down_live = (
        jnp.arange(down_slots, dtype=jnp.int32)[None, None, :] < down_count[:, :, None]
    ).astype(jnp.bfloat16)
    up_w = up_blocks * up_live[:, :, None, None]
    down_w = down_blocks * down_live[:, :, :, None, None]
    n_up = up_w.size
    n_down = down_w.size
    ints = jnp.concatenate(
        [up_rows.reshape(-1), down_rows.reshape(-1)]
    ).astype(jnp.bfloat16)
    n_ints = ints.shape[0]
    pad = (-n_ints) % LANES
    packed = jnp.concatenate(
        [up_w.reshape(-1), down_w.reshape(-1), ints, jnp.zeros((pad,), jnp.bfloat16)]
    ).reshape(1, -1, LANES)
    gathered_w = lax.all_gather(packed, "core", axis=0, tiled=True)
    gathered_w = permute_gather(gathered_w, "zhi")
    gathered_w = permute_gather(gathered_w, "y")
    groups = gathered_w.shape[0]
    flat = gathered_w.reshape(groups, -1)
    up_all = flat[:, :n_up].reshape(groups * up_blocks.shape[0], up_slots, BLK, BLK)
    down_all = flat[:, n_up : n_up + n_down].reshape(groups * down_cols, down_slots, BLK, BLK)
    ints_all = flat[:, n_up + n_down : n_up + n_down + n_ints].astype(jnp.int32)
    up_rows_all = ints_all[:, : up_rows.size].reshape(groups * up_blocks.shape[0], up_slots)
    down_rows_all = ints_all[:, up_rows.size :].reshape(groups * down_cols, down_slots)

    gathered = permute_gather(normed, "zlo")
    gathered = lax.all_gather(gathered, "x", axis=0, tiled=True)
    total_rows = gathered.shape[0]
    row_blocks = gathered.reshape(total_rows, D // BLK, BLK)

    dense_up = onehot_dense(up_all, up_rows_all, D // BLK)
    pre = jnp.einsum("tbk,cbkn->tcn", row_blocks, dense_up, preferred_element_type=jnp.float32)
    hidden = jax.nn.gelu(pre, approximate=True).astype(jnp.bfloat16)

    panel_span = FF // BLK // (lax.axis_size("x") * lax.axis_size("zlo"))
    dense_down = onehot_dense(down_all, down_rows_all, panel_span)
    partial_sums = jnp.einsum(
        "thi,jhin->tjn", hidden, dense_down, preferred_element_type=jnp.float32
    ).reshape(total_rows, D)
    summed = lax.psum_scatter(
        partial_sums.astype(jnp.bfloat16), "x", scatter_dimension=0, tiled=True
    )
    summed = permute_reduce_scatter(summed, "zlo")
    return (x_float + summed).astype(jnp.bfloat16)


def solution(mesh):
    fsdp = ("y", "zhi", "core")
    tp = ("x", "zlo")
    n_fsdp, n_tp = mesh.shape["fsdp"], mesh.shape["tp"]
    sizes = (n_fsdp // 4, 2, 2, n_tp // 4, 4)
    fine = Mesh(mesh.devices.reshape(sizes), fsdp + tp)
    placed = (
        P(fsdp + tp, None),
        P(),
        P(tp + fsdp, None, None, None),
        P(tp + fsdp, None),
        P(tp + fsdp),
        P(tp, fsdp, None, None, None),
        P(tp, fsdp, None),
        P(tp, fsdp),
    )
    return jax.shard_map(
        on_device, mesh=fine, in_specs=placed, out_specs=P(fsdp + tp, None), check_vma=False
    )
```

```python
import jax
import jax.numpy as jnp
from jax import lax
from jax.sharding import Mesh, PartitionSpec as P

D = 4096
FF = 16384
BLK = 64
LANES = 128


def onehot_dense(weights, rows, span):
    block_ids = jnp.arange(span, dtype=jnp.int32)
    onehot = (rows[:, :, None] == block_ids[None, None, :]).astype(jnp.bfloat16)
    dense = jnp.einsum("csb,cskn->cbkn", onehot, weights, preferred_element_type=jnp.float32)
    return dense.astype(jnp.bfloat16)


def permute_gather(piece, axis):
    size = lax.axis_size(axis)
    me = lax.axis_index(axis)
    whole = jnp.zeros((size,) + piece.shape, piece.dtype)
    whole = lax.dynamic_update_index_in_dim(whole, piece, me, 0)
    for shift in range(1, size):
        moved = lax.ppermute(piece, axis, [(i, (i + shift) % size) for i in range(size)])
        whole = lax.dynamic_update_index_in_dim(whole, moved, (me - shift) % size, 0)
    return whole.reshape((size * piece.shape[0],) + piece.shape[1:])


def permute_reduce_scatter(whole, axis):
    size = lax.axis_size(axis)
    me = lax.axis_index(axis)
    chunks = whole.reshape((size, whole.shape[0] // size) + whole.shape[1:])
    acc = lax.dynamic_index_in_dim(chunks, me, 0, keepdims=False).astype(jnp.float32)
    for shift in range(1, size):
        send = lax.dynamic_index_in_dim(chunks, (me + shift) % size, 0, keepdims=False)
        moved = lax.ppermute(send, axis, [(i, (i + shift) % size) for i in range(size)])
        acc = acc + moved.astype(jnp.float32)
    return acc


def on_device(tokens, norm_gain, up_blocks, up_rows, up_count, down_blocks, down_rows, down_count):
    x_float = tokens.astype(jnp.float32)
    scale = lax.rsqrt(jnp.mean(x_float * x_float, axis=-1, keepdims=True) + 1e-05)
    normed = (x_float * scale * norm_gain).astype(jnp.bfloat16)

    up_slots = up_blocks.shape[1]
    down_cols, down_slots = down_blocks.shape[1], down_blocks.shape[2]
    up_live = (jnp.arange(up_slots, dtype=jnp.int32)[None, :] < up_count[:, None]).astype(jnp.bfloat16)
    down_live = (
        jnp.arange(down_slots, dtype=jnp.int32)[None, None, :] < down_count[:, :, None]
    ).astype(jnp.bfloat16)
    up_w = up_blocks * up_live[:, :, None, None]
    down_w = down_blocks * down_live[:, :, :, None, None]
    n_up = up_w.size
    n_down = down_w.size
    ints = jnp.concatenate(
        [up_rows.reshape(-1), down_rows.reshape(-1)]
    ).astype(jnp.bfloat16)
    n_ints = ints.shape[0]
    pad = (-n_ints) % LANES
    packed = jnp.concatenate(
        [up_w.reshape(-1), down_w.reshape(-1), ints, jnp.zeros((pad,), jnp.bfloat16)]
    ).reshape(1, -1, LANES)
    gathered_w = lax.all_gather(packed, "core", axis=0, tiled=True)
    gathered_w = permute_gather(gathered_w, "zhi")
    gathered_w = permute_gather(gathered_w, "y")
    groups = gathered_w.shape[0]
    flat = gathered_w.reshape(groups, -1)
    up_all = flat[:, :n_up].reshape(groups * up_blocks.shape[0], up_slots, BLK, BLK)
    down_all = flat[:, n_up : n_up + n_down].reshape(groups * down_cols, down_slots, BLK, BLK)
    ints_all = flat[:, n_up + n_down : n_up + n_down + n_ints].astype(jnp.int32)
    up_rows_all = ints_all[:, : up_rows.size].reshape(groups * up_blocks.shape[0], up_slots)
    down_rows_all = ints_all[:, up_rows.size :].reshape(groups * down_cols, down_slots)

    gathered = permute_gather(normed, "zlo")
    gathered = lax.all_gather(gathered, "x", axis=0, tiled=True)
    total_rows = gathered.shape[0]
    row_blocks = gathered.reshape(total_rows, D // BLK, BLK)

    dense_up = onehot_dense(up_all, up_rows_all, D // BLK)
    pre = jnp.einsum("tbk,cbkn->tcn", row_blocks, dense_up, preferred_element_type=jnp.float32)
    hidden = jax.nn.gelu(pre, approximate=True).astype(jnp.bfloat16)

    panel_span = FF // BLK // (lax.axis_size("x") * lax.axis_size("zlo"))
    dense_down = onehot_dense(down_all, down_rows_all, panel_span)
    partial_sums = jnp.einsum(
        "thi,jhin->tjn", hidden, dense_down, preferred_element_type=jnp.float32
    ).reshape(total_rows, D)
    summed = permute_reduce_scatter(partial_sums.astype(jnp.bfloat16), "x")
    summed = permute_reduce_scatter(summed, "zlo")
    return (x_float + summed).astype(jnp.bfloat16)


def solution(mesh):
    fsdp = ("y", "zhi", "core")
    tp = ("x", "zlo")
    n_fsdp, n_tp = mesh.shape["fsdp"], mesh.shape["tp"]
    sizes = (n_fsdp // 4, 2, 2, n_tp // 4, 4)
    fine = Mesh(mesh.devices.reshape(sizes), fsdp + tp)
    placed = (
        P(fsdp + tp, None),
        P(),
        P(tp + fsdp, None, None, None),
        P(tp + fsdp, None),
        P(tp + fsdp),
        P(tp, fsdp, None, None, None),
        P(tp, fsdp, None),
        P(tp, fsdp),
    )
    return jax.shard_map(
        on_device, mesh=fine, in_specs=placed, out_specs=P(fsdp + tp, None), check_vma=False
    )
```
